32 devices in a mesh: slab: 8 (over z, x), freq: 4 (over y, core).
Axes of the slice: x: 2, y: 2, z: 4, core: 2. Of those that a mesh axis runs over, the one named last changes fastest.
Arguments:
- partials: bfloat16 [8, 3, 2, 32, 32, 5, 256], P('slab', None, None, 'freq'), may hold values from -400 to 400
- rec_plane: int32 [8, 3, 2], P('slab'), may hold values from 0 to 1
- rec_count: int32 [8, 3], P('slab'), may hold values from 0 to 2, as said below
- rec_weight: bfloat16 [8, 3, 2, 256], P('slab'), may hold values from 0.25 to 1
- qweight: float32 [16, 256], P('slab'), as said below
Outputs:
- spectra: bfloat16 [8, 32, 2, 16, 5, 256], P('freq', None, None, 'slab')
- r_factor: float32 [8, 64, 64], P('freq')
The draws below stay inside these ranges and needn't reach their ends.
Inputs may be any that keep to these rules, and one draw needn't show every extreme that they name: `rec_count`: at most 2 live records from one source to one destination, reached in every draw; a source's records to its own index number exactly 2; none leave the ends of the slab axis; some destination receives 2 from each of its three sources. `qweight`: positive.
All inputs are finite; a program needn't handle non-finite values.
Results may differ from the reference program's by a relative error of at most 0.0025.
The reference program's roundings to bfloat16 on the way count: a program that leaves them out, or rounds other values in their place, can miss the bound.
Values may be sent and summed in bfloat16 or wider, within the bound.
No kernel may reach another device: no remote copies, remote signals or barrier semaphores. Data moves between devices by JAX's collectives and lax.ppermute only.
A program may use at most 64 MiB of HBM per device.

```python
import math
import jax
import jax.numpy as jnp
from jax import lax

NV = 5
NT = 32
NBLK = 32
NY = 16
NZ = 16
SX = 2
CAP = 2
NF = 8
NCOL = 64
PTS = 256
NSRC = 8
NXG = 16


def draw_partials(key, part):
    first, second, third, fourth, fifth = jax.random.split(key, 5)
    shape = (NSRC, 3, CAP, NBLK, NT, NV, PTS)
    own_part = jnp.clip(jax.random.normal(first, shape, jnp.float32), -5.0, 5.0)
    shared = 0.7
    common = jnp.clip(jax.random.normal(second, (NSRC, 3, CAP, 1, NT, NV, PTS), jnp.float32), -5.0, 5.0)
    column_scale = jnp.exp(jax.random.uniform(third, (1, 1, 1, NBLK, 1, 1, 1), jnp.float32, minval=-1.15, maxval=1.15))
    variable_scale = jnp.exp(jax.random.uniform(fourth, (1, 1, 1, 1, 1, NV, 1), jnp.float32, minval=-1.15, maxval=1.15))
    picks = jax.random.permutation(fifth, NBLK) % NSRC
    source = jnp.arange(NSRC) % NBLK
    heavy = (source[:, None] == picks[None, :]).astype(jnp.float32)
    boost = (1.0 + 3.0 * heavy).reshape(NSRC, 1, 1, NBLK, 1, 1, 1)
    values = (own_part + shared * common) * column_scale * variable_scale * boost
    return values.astype(jnp.bfloat16)


def draw_rec_count(key, part):
    counts = jax.random.randint(key, (NSRC, 3), 1, CAP + 1)
    source = jnp.arange(NSRC)[:, None]
    side = jnp.arange(3)[None, :]
    counts = jnp.where(side == 1, CAP, counts)
    counts = jnp.where(source < 3, CAP, counts)
    counts = jnp.where((side == 0) & (source == 0), 0, counts)
    counts = jnp.where((side == 2) & (source == NSRC - 1), 0, counts)
    return counts.astype(jnp.int32)


def draw_qweight(key, part):
    planes = jnp.arange(NXG).astype(jnp.float32)[:, None]
    rise = jnp.exp(math.log(3.0) * planes / NXG)
    top = math.log(10.0)
    rough = jnp.exp(jax.random.uniform(key, (NXG, PTS), jnp.float32, minval=0.0, maxval=top))
    return (rise * rough / (6.0 * NXG * PTS)).astype(jnp.float32)


def with_ends(values, rng, smallest, high):
    shape = values.shape
    index_at = [jax.random.randint(jax.random.fold_in(rng, axis), (), 0, shape[axis]) for axis in range(len(shape))]
    values = values.at[tuple(index_at)].set(smallest)
    longest = shape.index(max(shape))
    index_at[longest] = (index_at[longest] + 1) % shape[longest]
    return values.at[tuple(index_at)].set(high)


def level_of(key, dims, cuts, smallest, largest):
    factor_of = 1.0
    for axis_at, parts in cuts:
        draws = jax.random.uniform(jax.random.fold_in(jax.random.fold_in(key, 6), axis_at), (parts,), jnp.float32, smallest / len(cuts), largest / len(cuts))
        factor_of = factor_of * jnp.repeat(jnp.exp(draws), dims[axis_at] // parts).reshape((-1,) + (1,) * (len(dims) - 1 - axis_at))
    return factor_of


def setup_inputs(seed: int = 0) -> dict:
    key_of = jax.random.split(jax.random.key(seed), 6)
    partials = draw_partials(jax.random.fold_in(key_of[5], 71), 0)
    rec_plane = with_ends(jax.random.randint(key_of[1], (NSRC, 3, CAP), 0, SX), jax.random.fold_in(key_of[1], 1), 0, SX - 1).astype(jnp.int32)
    rec_count = draw_rec_count(jax.random.fold_in(key_of[5], 71), 0)
    rec_weight = jnp.clip(jnp.exp(math.log(1.0) - 1.3862944 * jax.random.uniform(key_of[3], (NSRC, 3, CAP, PTS), jnp.float32) ** level_of(key_of[3], (NSRC, 3, CAP, PTS), ((0, 8),), -0.2, 0.2)), 0.25, 1.0).astype(jnp.bfloat16)
    qweight = draw_qweight(jax.random.fold_in(key_of[5], 71), 0)
    return dict(partials=partials, rec_plane=rec_plane, rec_count=rec_count, rec_weight=rec_weight, qweight=qweight)


TAPS = (-0.0625, 0.25, 0.625, 0.25, -0.0625)

def band_matrix(size):
    index = jnp.arange(size)
    offset = index[None, :] - index[:, None]
    result = jnp.zeros((size, size), jnp.float32)
    for place in range(5):
        result = result + TAPS[place] * (offset == place - 2).astype(jnp.float32)
    return result

def dft_table():
    times = jnp.arange(NT).astype(jnp.float32)
    freqs = jnp.arange(NF).astype(jnp.float32) + 1.0
    window = 0.5 - 0.5 * jnp.cos(2.0 * math.pi * times / NT)
    factor = 1.0 / jnp.sqrt(jnp.sum(window * window))
    angle = 2.0 * math.pi * times[:, None] * freqs[None, :] / NT
    real_part = factor * window[:, None] * jnp.cos(angle)
    imag_part = -factor * window[:, None] * jnp.sin(angle)
    return jnp.stack([real_part, imag_part], axis=2)

def reference(partials, rec_plane, rec_count, rec_weight, qweight):
    source = jnp.arange(NSRC)[:, None, None]
    side = jnp.arange(3)[None, :, None]
    slots = jnp.arange(CAP)[None, None, :]
    target = (source + side - 1) * SX + rec_plane
    valid = slots < rec_count[:, :, None]
    target = jnp.where(valid, target, NXG).reshape(-1).astype(jnp.int32)
    weights = rec_weight.reshape(-1, PTS).astype(jnp.float32)
    kyz = jnp.kron(band_matrix(NY), band_matrix(NZ)).astype(jnp.bfloat16)
    table = dft_table()

    def one_block(block):
        piece = lax.dynamic_index_in_dim(partials, block, 3, keepdims=False)
        scaled = piece.reshape(-1, NT, NV, PTS).astype(jnp.float32) * weights[:, None, None, :]
        grid = jax.ops.segment_sum(scaled, target, num_segments=NXG + 1)[:NXG].astype(jnp.bfloat16)
        padded = jnp.pad(grid, ((2, 2), (0, 0), (0, 0), (0, 0)))
        across = jnp.dot(padded.reshape(-1, PTS).astype(jnp.float32), kyz.astype(jnp.float32), preferred_element_type=jnp.float32)
        across = across.reshape(NXG + 4, NT, NV, PTS)
        smoothed = TAPS[0] * across[0:NXG]
        for place in range(1, 5):
            smoothed = smoothed + TAPS[place] * across[place:place + NXG]
        coeffs = jnp.einsum('xtvp,tkr->krxvp', smoothed, table, precision=lax.Precision.HIGHEST)
        return coeffs.astype(jnp.bfloat16)
    stacked = lax.map(one_block, jnp.arange(NBLK))
    spectra = jnp.transpose(stacked, (1, 0, 2, 3, 4, 5))

    def one_freq(freq):
        values = spectra[freq].astype(jnp.float32).reshape(NCOL, NXG, NV, PTS)
        weighted = (values * qweight[None, :, None, :]).reshape(NCOL, -1)
        return jnp.dot(weighted, values.reshape(NCOL, -1).T, precision=lax.Precision.HIGHEST)
    gram = lax.map(one_freq, jnp.arange(NF))
    r_factor = jnp.swapaxes(jnp.linalg.cholesky(gram), 1, 2)
    return (spectra, r_factor)
```

```python
import math

import jax
import jax.numpy as jnp
import numpy as np
from jax import lax
from jax.experimental import pallas as pl
from jax.experimental.pallas import tpu as pltpu
from jax.sharding import PartitionSpec as P

NY = 16
NZ = 16
NF = 8
TAPS = (-0.0625, 0.25, 0.625, 0.25, -0.0625)
BF16 = jnp.bfloat16
F32 = jnp.float32
F16_LOG2 = 14
LOW_LOG2 = -100


def band_matrix(size):
    offset = np.arange(size)[None, :] - np.arange(size)[:, None]
    return sum(TAPS[place] * (offset == place - 2) for place in range(5))


def plane_filter():
    return jnp.asarray(np.kron(band_matrix(NY), band_matrix(NZ)).astype(np.float32), BF16)


def two_parts(value):
    high = value.astype(BF16)
    return high, (value - high.astype(F32)).astype(BF16)


def dft_rows(blocks, times):
    t = np.arange(times)
    window = 0.5 - 0.5 * np.cos(2.0 * math.pi * t / times)
    factor = 1.0 / np.sqrt(np.sum(window * window))
    angle = 2.0 * math.pi * (np.arange(NF)[:, None] + 1.0) * t[None, :] / times
    table = factor * window * np.stack([np.cos(angle), -np.sin(angle)], axis=1)
    rows = np.einsum("krt,bc->kbrct", table, np.eye(blocks))
    rows = rows.reshape(NF * blocks * 2, blocks * times).astype(np.float32)
    high = rows.astype(jnp.bfloat16)
    low = (rows - high.astype(np.float32)).astype(jnp.bfloat16)
    return jnp.asarray(np.concatenate([high, low], axis=0))


def scale_table():
    e = np.arange(128) + LOW_LOG2
    power = np.exp2(e.astype(np.float64))
    factor = np.exp2((F16_LOG2 - e).astype(np.float64))
    rows = np.zeros((8, 128), np.float32)
    rows[0], rows[1], rows[2] = power, factor, e / factor
    return jnp.asarray(rows)


def weight_rows(weight_ref, plane_ref, count_ref, side, plane_total):
    cap = weight_ref.shape[2]
    rows = []
    for q in range(plane_total):
        for c in range(cap):
            live = (plane_ref[0, c, side] == q) & (c < count_ref[0, side])
            row = weight_ref[0, side, c : c + 1, :].astype(F32)
            rows.append(row * jnp.where(live, 1.0, 0.0))
    return rows


def pack_body(plane_total, partials, weight, plane, count, near, far, hold, tail, sems):
    parity = lax.rem(lax.axis_index("slab"), 2)
    pieces = near.shape[0] - 1
    points = near.shape[2]
    loads, stores = [], []
    for place, side in enumerate((1, 2 * parity)):
        load = pltpu.make_async_copy(partials.at[0, side], hold.at[place], sems.at[place])
        load.start()
        loads.append(load)
    for place, (side, target) in enumerate(((1, near), (2 * parity, far))):
        rows = weight_rows(weight, plane, count, side, plane_total)
        filler = jnp.zeros((tail.shape[1] - len(rows), points), F32)
        tail[place] = jnp.concatenate(rows + [filler], axis=0).astype(BF16)
    for place, target in enumerate((near, far)):
        store = pltpu.make_async_copy(tail.at[place], target.at[pieces], sems.at[4 + place])
        store.start()
        stores.append(store)
    for place, target in enumerate((near, far)):
        loads[place].wait()
        store = pltpu.make_async_copy(
            hold.at[place], target.at[pl.ds(0, pieces)], sems.at[2 + place]
        )
        store.start()
        stores.append(store)
    for store in stores:
        store.wait()


def assemble_body(
    dims, partials, weight, plane, count, near, far, dft, kyz, scales, out, factor_out, own, grid, sem
):
    plane_total, cap, blocks, variables, times, points = dims
    parity = lax.rem(lax.axis_index("slab"), 2)
    side = 2 - 2 * parity
    load = pltpu.make_async_copy(partials.at[0, side], own, sem)
    load.start()
    pieces = cap * blocks * variables
    own_rows = weight_rows(weight, plane, count, side, plane_total)
    near_rows = near[pieces].astype(F32)
    far_rows = far[pieces].astype(F32)
    load.wait()
    rows = dft.shape[0] // 2

    def one_variable(v, largest):
        for b in range(blocks):
            totals = [None] * plane_total
            for c in range(cap):
                place = (c * blocks + b) * variables + v
                terms = (own[place], near[place], far[place])
                for at, term in enumerate(terms):
                    value = term.astype(F32)
                    for q in range(plane_total):
                        index = q * cap + c
                        row = (
                            own_rows[index],
                            near_rows[index : index + 1],
                            far_rows[index : index + 1],
                        )[at]
                        product = value * row
                        totals[q] = product if totals[q] is None else totals[q] + product
            for q in range(plane_total):
                grid[q, b * times : (b + 1) * times, :] = totals[q].astype(BF16)
        for q in range(plane_total):
            both = jnp.dot(dft[...], grid[q], preferred_element_type=F32)
            high, low = two_parts(both[:rows] + both[rows:])
            both = jnp.dot(
                jnp.concatenate([high, low], axis=0), kyz[...], preferred_element_type=F32
            )
            coeffs = both[:rows] + both[rows:]
            start = pl.multiple_of((q * variables + v) * rows, rows)
            out[pl.ds(start, rows), :] = coeffs
            for i in range(0, rows, 8):
                largest = jnp.maximum(largest, jnp.abs(coeffs[i : i + 8]))
        return largest

    largest = lax.fori_loop(0, variables, one_variable, jnp.zeros((8, points), F32))
    largest = jnp.max(jnp.max(largest, axis=1, keepdims=True), axis=0, keepdims=True)
    passed = jnp.sum((largest >= scales[0:1, :]).astype(F32), axis=1, keepdims=True)
    lane = lax.broadcasted_iota(jnp.int32, (1, 128), 1).astype(F32)
    hit = lane == passed
    factor = jnp.sum(jnp.where(hit, scales[1:2, :], 0.0), axis=1, keepdims=True)
    mark = jnp.sum(jnp.where(hit, scales[2:3, :], 0.0), axis=1, keepdims=True)
    total = plane_total * variables * rows
    out[total : total + 16, :] = jnp.broadcast_to(mark, (16, points))
    factor_out[...] = jnp.broadcast_to(factor, (8, 128))


def gram_body(values, qweight, out):
    sources, freqs, planes, variables, rows, points = values.shape
    columns = sources * rows
    results = []
    for k in range(freqs):
        total = jnp.zeros((3 * columns, columns), F32)
        for x in range(planes):
            for v in range(variables):
                block = values[:, k, x, v].reshape(columns, points)
                weighted = block.astype(F32) * qweight[x : x + 1, :]
                high, low = two_parts(weighted)
                rest = weighted - high.astype(F32) - low.astype(F32)
                stack = jnp.concatenate([high, low, rest.astype(BF16)], axis=0)
                total = total + lax.dot_general(
                    stack, block, (((1,), (1,)), ((), ())), preferred_element_type=F32
                )
        results.append(total[:columns] + total[columns : 2 * columns] + total[2 * columns :])
    out[...] = jnp.concatenate(results, axis=1)


def factor_body(kept, grams, out):
    columns = grams.shape[1]
    total = jnp.sum(grams[...], axis=0)
    lane = lax.broadcasted_iota(jnp.int32, (8, columns), 1)
    sublane = lax.broadcasted_iota(jnp.int32, (8, columns), 0)
    for start in range(0, columns, 8):
        height = columns - start
        stripes = []
        for t in range(8):
            parts = [
                jnp.broadcast_to(
                    total[:, k * columns + start + t : k * columns + start + t + 1],
                    (height, columns),
                )
                for k in range(kept)
            ]
            stripes.append(jnp.concatenate(parts, axis=1))
        panel = total[:8]
        rows = []
        for t in range(8):
            inverse = lax.rsqrt(stripes[t][t : t + 1])
            stripes[t] = stripes[t] * inverse
            row = panel[t : t + 1] * inverse
            rows.append(row)
            for u in range(t + 1, 8):
                stripes[u] = stripes[u] - stripes[t] * stripes[t][u : u + 1]
            panel = panel - stripes[t][:8] * row
        block = jnp.concatenate(rows, axis=0)
        for k in range(kept):
            piece = block[:, k * columns : (k + 1) * columns]
            out[k, start : start + 8, :] = jnp.where(lane >= sublane + start, piece, 0.0)
        if height > 8:
            total = total[8:]
            for t in range(8):
                total = total - stripes[t][8:] * rows[t]


def pairs(count, even_step, odd_step):
    result = []
    for source in range(count):
        target = source + (odd_step if source % 2 else even_step)
        if 0 <= target < count:
            result.append((source, target))
    return result


def body(partials, rec_plane, rec_count, rec_weight, qweight):
    slabs = lax.axis_size("slab")
    freqs = lax.axis_size("freq")
    plane_total, points = qweight.shape
    _, _, cap, blocks, times, variables, _ = partials.shape
    pieces = cap * blocks * variables
    parity = lax.rem(lax.axis_index("slab"), 2)
    natural = jnp.transpose(partials, (0, 1, 2, 3, 5, 4, 6)).reshape(1, 3, pieces, times, points)
    planes = jnp.swapaxes(rec_plane, 1, 2)
    any_spec = pl.BlockSpec(memory_space=pl.ANY)
    vmem = pl.BlockSpec(memory_space=pltpu.VMEM)
    smem = pl.BlockSpec(memory_space=pltpu.SMEM)

    payload = jax.ShapeDtypeStruct((pieces + 1, times, points), BF16)
    near, far = pl.pallas_call(
        lambda *refs: pack_body(plane_total, *refs),
        out_shape=(payload, payload),
        in_specs=[any_spec, vmem, smem, smem],
        out_specs=(any_spec, any_spec),
        scratch_shapes=[
            pltpu.VMEM((2, pieces, times, points), BF16),
            pltpu.VMEM((2, times, points), BF16),
            pltpu.SemaphoreType.DMA((6,)),
        ],
        name="pack",
    )(natural, rec_weight, planes, rec_count)
    near = lax.ppermute(near, "slab", pairs(slabs, 1, -1))
    far = lax.ppermute(far, "slab", pairs(slabs, -2, 2))

    rows = 2 * NF * blocks
    total = plane_total * variables * rows
    dims = (plane_total, cap, blocks, variables, times, points)
    coeffs, factor = pl.pallas_call(
        lambda *refs: assemble_body(dims, *refs),
        out_shape=(
            jax.ShapeDtypeStruct((total + 16, points), F32),
            jax.ShapeDtypeStruct((8, 128), F32),
        ),
        in_specs=[any_spec, vmem, smem, smem] + [vmem] * 5,
        out_specs=(vmem, vmem),
        scratch_shapes=[
            pltpu.VMEM((pieces, times, points), BF16),
            pltpu.VMEM((plane_total, blocks * times, points), BF16),
            pltpu.SemaphoreType.DMA,
        ],
        name="assemble",
    )(
        natural,
        rec_weight,
        planes,
        rec_count,
        near,
        far,
        dft_rows(blocks, times),
        plane_filter(),
        scale_table(),
    )
    message = (coeffs * factor[0, 0]).astype(jnp.float16)
    middle = lax.ppermute(message, "slab", pairs(slabs, 1, -1))
    beyond = lax.ppermute(message, "slab", pairs(slabs, 2, -2))

    split = (plane_total, variables, NF, 2 * blocks, points)

    def opened(value):
        scale = jnp.exp2(value[total, 0].astype(F32) - F16_LOG2)
        return value[:total].astype(F32).reshape(split) * scale

    own = coeffs[:total].reshape(split)
    mid = opened(middle)
    outer = opened(beyond)
    low = jnp.where(parity == 0, outer, own)
    high = jnp.where(parity == 0, own, outer)
    line = [low[plane_total - 2], low[plane_total - 1]]
    line += [mid[x] for x in range(plane_total)] + [high[0], high[1]]
    local = []
    for x in range(plane_total):
        value = TAPS[0] * line[x]
        for place in range(1, 5):
            value = value + TAPS[place] * line[x + place]
        local.append(jnp.swapaxes(value.astype(BF16), 0, 1))
    local = jnp.stack(local, axis=1)
    values = lax.all_to_all(local, "freq", split_axis=0, concat_axis=0, tiled=True)
    kept = NF // freqs
    values = values.reshape(freqs, kept, plane_total, variables, 2 * blocks, points)
    columns = 2 * blocks * freqs
    gram = pl.pallas_call(
        gram_body,
        out_shape=jax.ShapeDtypeStruct((columns, kept * columns), F32),
        in_specs=[vmem, vmem],
        out_specs=vmem,
        name="gram",
    )(values, qweight)
    spread = jnp.broadcast_to(gram[None], (slabs,) + gram.shape)
    grams = lax.all_to_all(spread, "slab", split_axis=0, concat_axis=0, tiled=True)
    factor = pl.pallas_call(
        lambda *refs: factor_body(kept, *refs),
        out_shape=jax.ShapeDtypeStruct((kept, columns, columns), F32),
        in_specs=[vmem],
        out_specs=vmem,
        name="factor",
    )(grams)
    spectra = values.reshape(freqs, kept, plane_total, variables, blocks, 2, points)
    spectra = jnp.transpose(spectra, (1, 0, 4, 5, 2, 3, 6))
    spectra = spectra.reshape(kept, freqs * blocks, 2, plane_total, variables, points)
    return (spectra, factor)


def solution(mesh):
    placed = (
        P("slab", None, None, "freq", None, None, None),
        P("slab", None, None),
        P("slab", None),
        P("slab", None, None, None),
        P("slab", None),
    )
    return jax.shard_map(
        body,
        mesh=mesh,
        in_specs=placed,
        out_specs=(P("freq", None, None, "slab", None, None), P("freq", None, None)),
        check_vma=False,
    )
```

```python
import math

import jax
import jax.numpy as jnp
import numpy as np
from jax import lax
from jax.experimental import pallas as pl
from jax.experimental.pallas import tpu as pltpu
from jax.sharding import PartitionSpec as P

NY = 16
NZ = 16
NF = 8
TAPS = (-0.0625, 0.25, 0.625, 0.25, -0.0625)
BF16 = jnp.bfloat16
F32 = jnp.float32
F16_LOG2 = 14
LOW_LOG2 = -100
PARAMS = pltpu.CompilerParams(vmem_limit_bytes=24 << 20)


def band_matrix(size):
    offset = np.arange(size)[None, :] - np.arange(size)[:, None]
    return sum(TAPS[place] * (offset == place - 2) for place in range(5))


def plane_filter():
    return jnp.asarray(np.kron(band_matrix(NY), band_matrix(NZ)).astype(np.float32), BF16)


def two_parts(value):
    high = value.astype(BF16)
    return high, (value - high.astype(F32)).astype(BF16)


def dft_rows(blocks, times):
    t = np.arange(times)
    window = 0.5 - 0.5 * np.cos(2.0 * math.pi * t / times)
    factor = 1.0 / np.sqrt(np.sum(window * window))
    angle = 2.0 * math.pi * (np.arange(NF)[:, None] + 1.0) * t[None, :] / times
    table = factor * window * np.stack([np.cos(angle), -np.sin(angle)], axis=1)
    rows = np.einsum("krt,bc->kbrct", table, np.eye(blocks))
    rows = rows.reshape(NF * blocks * 2, blocks * times).astype(np.float32)
    high = rows.astype(jnp.bfloat16)
    low = (rows - high.astype(np.float32)).astype(jnp.bfloat16)
    return jnp.asarray(np.concatenate([high, low], axis=0))


def scale_table():
    e = np.arange(128) + LOW_LOG2
    power = np.exp2(e.astype(np.float64))
    factor = np.exp2((F16_LOG2 - e).astype(np.float64))
    rows = np.zeros((8, 128), np.float32)
    rows[0], rows[1], rows[2] = power, factor, e / factor
    return jnp.asarray(rows)


def weight_rows(weight_ref, plane_ref, count_ref, side, plane_total):
    cap = weight_ref.shape[2]
    rows = []
    for q in range(plane_total):
        for c in range(cap):
            live = (plane_ref[0, c, side] == q) & (c < count_ref[0, side])
            row = weight_ref[0, side, c : c + 1, :].astype(F32)
            rows.append(row * jnp.where(live, 1.0, 0.0))
    return rows


def pack_body(chunk, plane_total, partials, weight, plane, count, near, far, hold, tail, sems):
    first, width = chunk
    parity = lax.rem(lax.axis_index("slab"), 2)
    groups = hold.shape[1]
    sides = (1, 2 * parity)
    loads, stores = [], []
    for place, side in enumerate(sides):
        load = pltpu.make_async_copy(
            partials.at[0, side, :, pl.ds(first, width)], hold.at[place], sems.at[place, groups]
        )
        load.start()
        loads.append(load)
    for place, (side, target) in enumerate(zip(sides, (near, far))):
        rows = weight_rows(weight, plane, count, side, plane_total)
        filler = jnp.zeros((tail.shape[1] - len(rows), tail.shape[2]), F32)
        tail[place] = jnp.concatenate(rows + [filler], axis=0).astype(BF16)
    for place, target in enumerate((near, far)):
        loads[place].wait()
        for g in range(groups):
            store = pltpu.make_async_copy(
                hold.at[place, g], target.at[pl.ds(g * width, width)], sems.at[place, g]
            )
            store.start()
            stores.append(store)
        store = pltpu.make_async_copy(
            tail.at[place], target.at[groups * width], sems.at[place, groups + 1]
        )
        store.start()
        stores.append(store)
    for store in stores:
        store.wait()


def tap_sums(plane_total, start):
    table = []
    for x in range(plane_total):
        places = [start + q - x for q in range(plane_total)]
        table.append([TAPS[at] if 0 <= at < 5 else 0.0 for at in places])
    return table


def assemble_body(
    dims, partials, weight, plane, count, near, far, dft, kyz, scales,
    kept_out, mid_out, outer_out, factor_out, own, near_hold, far_hold, grid, sems,
):
    first, width, plane_total, cap, blocks, times, points = dims
    parity = lax.rem(lax.axis_index("slab"), 2)
    even = parity == 0
    side = 2 - 2 * parity
    loads = [
        pltpu.make_async_copy(
            partials.at[0, side, :, pl.ds(first, width)], own, sems.at[0]
        ),
        pltpu.make_async_copy(near, near_hold, sems.at[1]),
        pltpu.make_async_copy(far, far_hold, sems.at[2]),
    ]
    for load in loads:
        load.start()
    pieces = cap * blocks * width
    own_rows = weight_rows(weight, plane, count, side, plane_total)
    for load in loads:
        load.wait()
    near_rows = near_hold[pieces].astype(F32)
    far_rows = far_hold[pieces].astype(F32)
    rows = dft.shape[0] // 2
    height = 2 * blocks
    low = tap_sums(plane_total, 2 - plane_total)
    mid = tap_sums(plane_total, 2)
    high = tap_sums(plane_total, 2 + plane_total)
    largest = jnp.zeros((8, points), F32)
    for v in range(width):
        for b in range(blocks):
            totals = [None] * plane_total
            for c in range(cap):
                group = c * blocks + b
                terms = (own[group, v], near_hold[group * width + v], far_hold[group * width + v])
                for at, term in enumerate(terms):
                    value = term.astype(F32)
                    for q in range(plane_total):
                        index = q * cap + c
                        row = (
                            own_rows[index],
                            near_rows[index : index + 1],
                            far_rows[index : index + 1],
                        )[at]
                        product = value * row
                        totals[q] = product if totals[q] is None else totals[q] + product
            for q in range(plane_total):
                grid[q, b * times : (b + 1) * times, :] = totals[q].astype(BF16)
        coeffs = []
        for q in range(plane_total):
            both = jnp.dot(dft[...], grid[q], preferred_element_type=F32)
            high_part, low_part = two_parts(both[:rows] + both[rows:])
            both = jnp.dot(
                jnp.concatenate([high_part, low_part], axis=0),
                kyz[...],
                preferred_element_type=F32,
            )
            coeffs.append(both[:rows] + both[rows:])
        for x in range(plane_total):
            kept = sent = middle = 0.0
            for q in range(plane_total):
                lower, upper = low[x][q], high[x][q]
                kept = kept + coeffs[q] * jnp.where(even, upper, lower)
                sent = sent + coeffs[q] * jnp.where(even, lower, upper)
                middle = middle + coeffs[q] * mid[x][q]
            for i in range(0, rows, 8):
                part = jnp.maximum(jnp.abs(sent[i : i + 8]), jnp.abs(middle[i : i + 8]))
                largest = jnp.maximum(largest, part)
            for k in range(rows // height):
                start = ((k * plane_total + x) * width + v) * height
                for target, value in ((kept_out, kept), (mid_out, middle), (outer_out, sent)):
                    target[start : start + height, :] = value[k * height : (k + 1) * height]
    largest = jnp.max(jnp.max(largest, axis=1, keepdims=True), axis=0, keepdims=True)
    passed = jnp.sum((largest >= scales[0:1, :]).astype(F32), axis=1, keepdims=True)
    lane = lax.broadcasted_iota(jnp.int32, (1, 128), 1).astype(F32)
    hit = lane == passed
    factor = jnp.sum(jnp.where(hit, scales[1:2, :], 0.0), axis=1, keepdims=True)
    mark = jnp.sum(jnp.where(hit, scales[2:3, :], 0.0), axis=1, keepdims=True)
    total = plane_total * width * rows
    for target in (mid_out, outer_out):
        target[total : total + 16, :] = jnp.broadcast_to(mark, (16, points))
    factor_out[...] = jnp.broadcast_to(factor, (8, 128))


def gram_body(values, qweight, *refs):
    *before, out = refs
    sources, freqs, planes, variables, rows, points = values.shape
    columns = sources * rows
    results = []
    for k in range(freqs):
        total = jnp.zeros((3 * columns, columns), F32)
        for x in range(planes):
            for v in range(variables):
                block = values[:, k, x, v].reshape(columns, points)
                weighted = block.astype(F32) * qweight[x : x + 1, :]
                high, low = two_parts(weighted)
                rest = weighted - high.astype(F32) - low.astype(F32)
                stack = jnp.concatenate([high, low, rest.astype(BF16)], axis=0)
                total = total + lax.dot_general(
                    stack, block, (((1,), (1,)), ((), ())), preferred_element_type=F32
                )
        results.append(total[:columns] + total[columns : 2 * columns] + total[2 * columns :])
    result = jnp.concatenate(results, axis=1)
    for earlier in before:
        result = result + earlier[0]
    for copy in range(out.shape[0]):
        out[copy] = result


def factor_body(kept, grams, out):
    columns = grams.shape[1]
    total = jnp.sum(grams[...], axis=0)
    lane = lax.broadcasted_iota(jnp.int32, (8, columns), 1)
    sublane = lax.broadcasted_iota(jnp.int32, (8, columns), 0)
    for start in range(0, columns, 8):
        height = columns - start
        stripes = []
        for t in range(8):
            parts = [
                jnp.broadcast_to(
                    total[:, k * columns + start + t : k * columns + start + t + 1],
                    (height, columns),
                )
                for k in range(kept)
            ]
            stripes.append(jnp.concatenate(parts, axis=1))
        panel = total[:8]
        rows = []
        for t in range(8):
            inverse = lax.rsqrt(stripes[t][t : t + 1])
            stripes[t] = stripes[t] * inverse
            row = panel[t : t + 1] * inverse
            rows.append(row)
            for u in range(t + 1, 8):
                stripes[u] = stripes[u] - stripes[t] * stripes[t][u : u + 1]
            panel = panel - stripes[t][:8] * row
        block = jnp.concatenate(rows, axis=0)
        for k in range(kept):
            piece = block[:, k * columns : (k + 1) * columns]
            out[k, start : start + 8, :] = jnp.where(lane >= sublane + start, piece, 0.0)
        if height > 8:
            total = total[8:]
            for t in range(8):
                total = total - stripes[t][8:] * rows[t]


def pairs(count, even_step, odd_step):
    result = []
    for source in range(count):
        target = source + (odd_step if source % 2 else even_step)
        if 0 <= target < count:
            result.append((source, target))
    return result


def chunks_of(variables):
    head = (3 * variables + 2) // 5
    return [(0, head), (head, variables - head)] if head < variables else [(0, variables)]


def body(partials, rec_plane, rec_count, rec_weight, qweight):
    slabs = lax.axis_size("slab")
    freqs = lax.axis_size("freq")
    plane_total, points = qweight.shape
    _, _, cap, blocks, times, variables, _ = partials.shape
    groups = cap * blocks
    natural = jnp.transpose(partials, (0, 1, 2, 3, 5, 4, 6))
    natural = natural.reshape(1, 3, groups, variables, times, points)
    natural = pltpu.with_memory_space_constraint(natural, pltpu.HBM)
    planes = jnp.swapaxes(rec_plane, 1, 2)
    any_spec = pl.BlockSpec(memory_space=pl.ANY)
    hbm = pl.BlockSpec(memory_space=pltpu.HBM)
    vmem = pl.BlockSpec(memory_space=pltpu.VMEM)
    smem = pl.BlockSpec(memory_space=pltpu.SMEM)
    dft, kyz, scales = dft_rows(blocks, times), plane_filter(), scale_table()
    kept = NF // freqs
    height = 2 * blocks
    columns = height * freqs
    chunks = chunks_of(variables)

    def raw(chunk, weight):
        width = chunk[1]
        payload = jax.ShapeDtypeStruct((groups * width + 1, times, points), BF16)
        near, far = pl.pallas_call(
            lambda *refs: pack_body(chunk, plane_total, *refs),
            out_shape=(payload, payload),
            in_specs=[hbm, vmem, smem, smem],
            out_specs=(any_spec, any_spec),
            scratch_shapes=[
                pltpu.VMEM((2, groups, width, times, points), BF16),
                pltpu.VMEM((2, times, points), BF16),
                pltpu.SemaphoreType.DMA((2, groups + 2)),
            ],
            name="pack",
        )(natural, weight, planes, rec_count)
        weight, near, far = lax.optimization_barrier((weight, near, far))
        near = lax.ppermute(near, "slab", pairs(slabs, 1, -1))
        far = lax.ppermute(far, "slab", pairs(slabs, -2, 2))
        return weight, (near, far)

    def assembled(chunk, weight, near, far):
        width = chunk[1]
        total = NF * plane_total * width * height
        dims = chunk + (plane_total, cap, blocks, times, points)
        own, middle, outer, factor = pl.pallas_call(
            lambda *refs: assemble_body(dims, *refs),
            out_shape=(
                jax.ShapeDtypeStruct((total, points), F32),
                jax.ShapeDtypeStruct((total + 16, points), F32),
                jax.ShapeDtypeStruct((total + 16, points), F32),
                jax.ShapeDtypeStruct((8, 128), F32),
            ),
            in_specs=[hbm, vmem, smem, smem, any_spec, any_spec] + [vmem] * 3,
            out_specs=(vmem,) * 4,
            scratch_shapes=[
                pltpu.VMEM((groups, width, times, points), BF16),
                pltpu.VMEM((groups * width + 1, times, points), BF16),
                pltpu.VMEM((groups * width + 1, times, points), BF16),
                pltpu.VMEM((plane_total, blocks * times, points), BF16),
                pltpu.SemaphoreType.DMA((3,)),
            ],
            compiler_params=PARAMS,
            name="assemble",
        )(natural, weight, planes, rec_count, near, far, dft, kyz, scales)
        middle, outer = (
            (value * factor[0, 0]).astype(jnp.float16) for value in (middle, outer)
        )
        weight, own, middle, outer = lax.optimization_barrier((weight, own, middle, outer))
        middle = lax.ppermute(middle, "slab", pairs(slabs, 1, -1))
        outer = lax.ppermute(outer, "slab", pairs(slabs, 2, -2))
        return weight, (own, middle, outer)

    def combined(chunk, token, own, middle, outer):
        width = chunk[1]
        total = own.shape[0]
        own, middle, outer, token = lax.optimization_barrier((own, middle, outer, token))
        for message in (middle, outer):
            scale = jnp.exp2(message[total : total + 1].astype(F32) - F16_LOG2)
            own = own + message[:total].astype(F32) * scale
        own = own.astype(BF16)
        local = own.reshape(NF, plane_total, width, height, points)
        values = lax.all_to_all(local, "freq", split_axis=0, concat_axis=0, tiled=True)
        return own, values.reshape(freqs, kept, plane_total, width, height, points)

    def partial_gram(values, before, copies):
        return pl.pallas_call(
            gram_body,
            out_shape=jax.ShapeDtypeStruct((copies, columns, kept * columns), F32),
            in_specs=[vmem] * (2 + len(before)),
            out_specs=vmem,
            compiler_params=PARAMS,
            name="gram",
        )(values, qweight, *before)

    arrived = []
    weight = rec_weight
    for chunk in chunks:
        weight, records = raw(chunk, weight)
        arrived.append(records)
    sent = []
    for chunk, records in zip(chunks, arrived):
        weight, parts = assembled(chunk, weight, *records)
        sent.append(parts)
    values = []
    token = qweight
    for chunk, parts in zip(chunks, sent):
        token, value = combined(chunk, token, *parts)
        values.append(value)
    gram = ()
    for at, value in enumerate(values):
        copies = slabs if at == len(values) - 1 else 1
        gram = (partial_gram(value, gram, copies),)
    grams = lax.all_to_all(gram[0], "slab", split_axis=0, concat_axis=0, tiled=True)
    factor = pl.pallas_call(
        lambda *refs: factor_body(kept, *refs),
        out_shape=jax.ShapeDtypeStruct((kept, columns, columns), F32),
        in_specs=[vmem],
        out_specs=vmem,
        compiler_params=PARAMS,
        name="factor",
    )(grams)
    spectra = jnp.concatenate(values, axis=3)
    spectra = spectra.reshape(freqs, kept, plane_total, variables, blocks, 2, points)
    spectra = jnp.transpose(spectra, (1, 0, 4, 5, 2, 3, 6))
    spectra = spectra.reshape(kept, freqs * blocks, 2, plane_total, variables, points)
    return (spectra, factor)


def solution(mesh):
    placed = (
        P("slab", None, None, "freq", None, None, None),
        P("slab", None, None),
        P("slab", None),
        P("slab", None, None, None),
        P("slab", None),
    )
    return jax.shard_map(
        body,
        mesh=mesh,
        in_specs=placed,
        out_specs=(P("freq", None, None, "slab", None, None), P("freq", None, None)),
        check_vma=False,
    )
```

```python
import math

import jax
import jax.numpy as jnp
import numpy as np
from jax import lax
from jax.experimental import pallas as pl
from jax.experimental.pallas import tpu as pltpu
from jax.sharding import PartitionSpec as P

NY = 16
NZ = 16
NF = 8
TAPS = (-0.0625, 0.25, 0.625, 0.25, -0.0625)
BF16 = jnp.bfloat16
F32 = jnp.float32
F16_LOG2 = 14
LOW_LOG2 = -100
PARAMS = pltpu.CompilerParams(vmem_limit_bytes=24 << 20)


def band_matrix(size):
    offset = np.arange(size)[None, :] - np.arange(size)[:, None]
    return sum(TAPS[place] * (offset == place - 2) for place in range(5))


def plane_filter():
    return jnp.asarray(np.kron(band_matrix(NY), band_matrix(NZ)).astype(np.float32), BF16)


def two_parts(value):
    high = value.astype(BF16)
    return high, (value - high.astype(F32)).astype(BF16)


def dft_rows(blocks, times):
    t = np.arange(times)
    window = 0.5 - 0.5 * np.cos(2.0 * math.pi * t / times)
    factor = 1.0 / np.sqrt(np.sum(window * window))
    angle = 2.0 * math.pi * (np.arange(NF)[:, None] + 1.0) * t[None, :] / times
    table = factor * window * np.stack([np.cos(angle), -np.sin(angle)], axis=1)
    rows = np.einsum("krt,bc->kbrct", table, np.eye(blocks))
    rows = rows.reshape(NF * blocks * 2, blocks * times).astype(np.float32)
    high = rows.astype(jnp.bfloat16)
    low = (rows - high.astype(np.float32)).astype(jnp.bfloat16)
    return jnp.asarray(np.concatenate([high, low], axis=0))


def scale_table():
    e = np.arange(128) + LOW_LOG2
    power = np.exp2(e.astype(np.float64))
    factor = np.exp2((F16_LOG2 - e).astype(np.float64))
    rows = np.zeros((8, 128), np.float32)
    rows[0], rows[1], rows[2] = power, factor, e / factor
    return jnp.asarray(rows)


def weight_rows(weight_ref, plane_ref, count_ref, side, plane_total):
    cap = weight_ref.shape[2]
    rows = []
    for q in range(plane_total):
        for c in range(cap):
            live = (plane_ref[0, c, side] == q) & (c < count_ref[0, side])
            row = weight_ref[0, side, c : c + 1, :].astype(F32)
            rows.append(row * jnp.where(live, 1.0, 0.0))
    return rows


def weights_body(plane_total, weight, plane, count, own, near, far):
    parity = lax.rem(lax.axis_index("slab"), 2)
    for side, target in ((2 - 2 * parity, own), (1, near), (2 * parity, far)):
        rows = weight_rows(weight, plane, count, side, plane_total)
        filler = jnp.zeros((target.shape[0] - len(rows), target.shape[1]), F32)
        target[...] = jnp.concatenate(rows + [filler], axis=0).astype(BF16)


def tap_sums(plane_total, start):
    table = []
    for x in range(plane_total):
        places = [start + q - x for q in range(plane_total)]
        table.append([TAPS[at] if 0 <= at < 5 else 0.0 for at in places])
    return table


def assemble_body(
    dims, partials, own_weight, near_weight, far_weight, near, far, dft, kyz, scales,
    kept_out, mid_out, outer_out, factor_out, own, near_hold, far_hold, grid, sems,
):
    first, width, plane_total, cap, blocks, times, points = dims
    parity = lax.rem(lax.axis_index("slab"), 2)
    even = parity == 0
    side = 2 - 2 * parity
    loads = [
        pltpu.make_async_copy(
            partials.at[0, side, :, pl.ds(first, width)], own, sems.at[0]
        ),
        pltpu.make_async_copy(near, near_hold, sems.at[1]),
        pltpu.make_async_copy(far, far_hold, sems.at[2]),
    ]
    for load in loads:
        load.start()
    weights = [ref[...].astype(F32) for ref in (own_weight, near_weight, far_weight)]
    for load in loads:
        load.wait()
    rows = dft.shape[0] // 2
    height = 2 * blocks
    low = tap_sums(plane_total, 2 - plane_total)
    mid = tap_sums(plane_total, 2)
    high = tap_sums(plane_total, 2 + plane_total)
    largest = jnp.zeros((8, points), F32)
    for v in range(width):
        for b in range(blocks):
            totals = [None] * plane_total
            for c in range(cap):
                group = c * blocks + b
                for at, ref in enumerate((own, near_hold, far_hold)):
                    value = ref[group, v].astype(F32)
                    for q in range(plane_total):
                        index = q * cap + c
                        row = weights[at][index : index + 1]
                        product = value * row
                        totals[q] = product if totals[q] is None else totals[q] + product
            for q in range(plane_total):
                grid[q, b * times : (b + 1) * times, :] = totals[q].astype(BF16)
        coeffs = []
        for q in range(plane_total):
            both = jnp.dot(dft[...], grid[q], preferred_element_type=F32)
            high_part, low_part = two_parts(both[:rows] + both[rows:])
            both = jnp.dot(
                jnp.concatenate([high_part, low_part], axis=0),
                kyz[...],
                preferred_element_type=F32,
            )
            coeffs.append(both[:rows] + both[rows:])
        for x in range(plane_total):
            kept = sent = middle = 0.0
            for q in range(plane_total):
                lower, upper = low[x][q], high[x][q]
                kept = kept + coeffs[q] * jnp.where(even, upper, lower)
                sent = sent + coeffs[q] * jnp.where(even, lower, upper)
                middle = middle + coeffs[q] * mid[x][q]
            for i in range(0, rows, 8):
                part = jnp.maximum(jnp.abs(sent[i : i + 8]), jnp.abs(middle[i : i + 8]))
                largest = jnp.maximum(largest, part)
            for k in range(rows // height):
                place = (k * plane_total + x) * width + v
                for target, value in ((kept_out, kept), (mid_out, middle), (outer_out, sent)):
                    target[place] = value[k * height : (k + 1) * height]
    largest = jnp.max(jnp.max(largest, axis=1, keepdims=True), axis=0, keepdims=True)
    passed = jnp.sum((largest >= scales[0:1, :]).astype(F32), axis=1, keepdims=True)
    lane = lax.broadcasted_iota(jnp.int32, (1, 128), 1).astype(F32)
    hit = lane == passed
    factor = jnp.sum(jnp.where(hit, scales[1:2, :], 0.0), axis=1, keepdims=True)
    mark = jnp.sum(jnp.where(hit, scales[2:3, :], 0.0), axis=1, keepdims=True)
    for target in (mid_out, outer_out):
        target[target.shape[0] - 1] = jnp.broadcast_to(mark, (height, points))
    factor_out[...] = jnp.broadcast_to(factor, (8, 128))


def partner(index, step, count):
    return index ^ step if count & (count - 1) == 0 else lax.rem(index + step, count)


def giver(index, step, count):
    return partner(index, step if count & (count - 1) == 0 else count - step, count)


def gram_body(pieces, *refs):
    blocks, qweight, before, (values, out) = (
        refs[:pieces], refs[pieces], refs[pieces + 1 : -2], refs[-2:],
    )
    me = lax.axis_index("freq")
    for step, block in enumerate(blocks):
        values[giver(me, step, pieces)] = block[...]
    sources, freqs, planes, variables, rows, points = values.shape
    columns = sources * rows
    results = []
    for k in range(freqs):
        total = jnp.zeros((3 * columns, columns), F32)
        for x in range(planes):
            for v in range(variables):
                block = values[:, k, x, v].reshape(columns, points)
                weighted = block.astype(F32) * qweight[x : x + 1, :]
                high, low = two_parts(weighted)
                rest = weighted - high.astype(F32) - low.astype(F32)
                stack = jnp.concatenate([high, low, rest.astype(BF16)], axis=0)
                total = total + lax.dot_general(
                    stack, block, (((1,), (1,)), ((), ())), preferred_element_type=F32
                )
        results.append(total[:columns] + total[columns : 2 * columns] + total[2 * columns :])
    result = jnp.concatenate(results, axis=1)
    for earlier in before:
        result = result + earlier[0]
    for copy in range(out.shape[0]):
        out[copy] = result


def factor_body(kept, grams, out):
    columns = grams.shape[1]
    total = jnp.sum(grams[...], axis=0)
    lane = lax.broadcasted_iota(jnp.int32, (8, columns), 1)
    sublane = lax.broadcasted_iota(jnp.int32, (8, columns), 0)
    for start in range(0, columns, 8):
        height = columns - start
        stripes = []
        for t in range(8):
            parts = [
                jnp.broadcast_to(
                    total[:, k * columns + start + t : k * columns + start + t + 1],
                    (height, columns),
                )
                for k in range(kept)
            ]
            stripes.append(jnp.concatenate(parts, axis=1))
        panel = total[:8]
        rows = []
        for t in range(8):
            inverse = lax.rsqrt(stripes[t][t : t + 1])
            stripes[t] = stripes[t] * inverse
            row = panel[t : t + 1] * inverse
            rows.append(row)
            for u in range(t + 1, 8):
                stripes[u] = stripes[u] - stripes[t] * stripes[t][u : u + 1]
            panel = panel - stripes[t][:8] * row
        block = jnp.concatenate(rows, axis=0)
        for k in range(kept):
            piece = block[:, k * columns : (k + 1) * columns]
            out[k, start : start + 8, :] = jnp.where(lane >= sublane + start, piece, 0.0)
        if height > 8:
            total = total[8:]
            for t in range(8):
                total = total - stripes[t][8:] * rows[t]


def pairs(count, even_step, odd_step):
    result = []
    for source in range(count):
        target = source + (odd_step if source % 2 else even_step)
        if 0 <= target < count:
            result.append((source, target))
    return result


def chunks_of(variables):
    head = (3 * variables + 2) // 5
    return [(0, head), (head, variables - head)] if head < variables else [(0, variables)]


def body(partials, rec_plane, rec_count, rec_weight, qweight):
    slabs = lax.axis_size("slab")
    freqs = lax.axis_size("freq")
    plane_total, points = qweight.shape
    _, _, cap, blocks, times, variables, _ = partials.shape
    groups = cap * blocks
    natural = jnp.transpose(partials, (0, 1, 2, 3, 5, 4, 6))
    natural = natural.reshape(1, 3, groups, variables, times, points)
    pinned = pltpu.with_memory_space_constraint(natural, pltpu.HBM)
    parity = lax.rem(lax.axis_index("slab"), 2)
    planes = jnp.swapaxes(rec_plane, 1, 2)
    any_spec = pl.BlockSpec(memory_space=pl.ANY)
    hbm = pl.BlockSpec(memory_space=pltpu.HBM)
    vmem = pl.BlockSpec(memory_space=pltpu.VMEM)
    smem = pl.BlockSpec(memory_space=pltpu.SMEM)
    dft, kyz, scales = dft_rows(blocks, times), plane_filter(), scale_table()
    kept = NF // freqs
    height = 2 * blocks
    columns = height * freqs
    chunks = chunks_of(variables)

    def raw(chunk, token):
        first, width = chunk
        shape = (1, 1, groups, width, times, points)
        near = lax.slice(natural, (0, 1, 0, first, 0, 0), (1, 2, groups, first + width, times, points))
        near, token = lax.optimization_barrier((near, token))
        far = lax.dynamic_slice(natural, (0, token, 0, first, 0, 0), shape)
        far, token = lax.optimization_barrier((far, token))
        return token, near.reshape(shape[2:]), far.reshape(shape[2:])

    def assembled(chunk, weights, near, far):
        width = chunk[1]
        total = NF * plane_total * width
        dims = chunk + (plane_total, cap, blocks, times, points)
        held = pltpu.VMEM((groups, width, times, points), BF16)
        message = jax.ShapeDtypeStruct((total + 1, height, points), F32)
        own, middle, outer, factor = pl.pallas_call(
            lambda *refs: assemble_body(dims, *refs),
            out_shape=(
                jax.ShapeDtypeStruct((total, height, points), F32),
                message,
                message,
                jax.ShapeDtypeStruct((8, 128), F32),
            ),
            in_specs=[hbm] + [vmem] * 3 + [any_spec] * 2 + [vmem] * 3,
            out_specs=(vmem,) * 4,
            scratch_shapes=[
                held,
                held,
                held,
                pltpu.VMEM((plane_total, blocks * times, points), BF16),
                pltpu.SemaphoreType.DMA((3,)),
            ],
            compiler_params=PARAMS,
            name="assemble",
        )(pinned, *weights, near, far, dft, kyz, scales)
        middle, outer = (
            (value * factor[0, 0]).astype(jnp.float16) for value in (middle, outer)
        )
        weights, own, middle, outer = lax.optimization_barrier((weights, own, middle, outer))
        middle = lax.ppermute(middle, "slab", swap)
        outer = lax.ppermute(outer, "slab", pairs(slabs, 2, -2))
        return weights, (own, middle, outer)

    def combined(chunk, token, own, middle, outer):
        width = chunk[1]
        own, middle, outer, token = lax.optimization_barrier((own, middle, outer, token))
        scales = [jnp.exp2(m[-1:, :1].astype(F32) - F16_LOG2) for m in (middle, outer)]
        size = kept * plane_total * width
        parts = []
        for step in range(freqs):
            start = partner(lax.axis_index("freq"), step, freqs) * size
            value = lax.dynamic_slice_in_dim(own, start, size, 0)
            for message, scale in zip((middle, outer), scales):
                value = value + lax.dynamic_slice_in_dim(message, start, size, 0) * scale
            parts.append(value.astype(BF16))
        parts = lax.optimization_barrier(tuple(parts))
        token = parts[0]
        arrived = []
        for step, value in enumerate(parts):
            if step:
                route = [(f, int(partner(np.int64(f), step, freqs))) for f in range(freqs)]
                value = lax.ppermute(value, "freq", route)
            arrived.append(value.reshape(kept, plane_total, width, height, points))
        return token, arrived

    def partial_gram(blocks, before, copies):
        return pl.pallas_call(
            lambda *refs: gram_body(freqs, *refs),
            out_shape=(
                jax.ShapeDtypeStruct((freqs,) + blocks[0].shape, BF16),
                jax.ShapeDtypeStruct((copies, columns, kept * columns), F32),
            ),
            in_specs=[vmem] * (freqs + 1 + len(before)),
            out_specs=(vmem, vmem),
            compiler_params=PARAMS,
            name="gram",
        )(*blocks, qweight, *before)

    swap = pairs(slabs, 1, -1)
    onward = pairs(slabs, -2, 2)
    arrived = []
    token = 2 * parity
    for chunk in chunks:
        token, near, far = raw(chunk, token)
        arrived.append((lax.ppermute(near, "slab", swap), lax.ppermute(far, "slab", onward)))
    small = jax.ShapeDtypeStruct((16, points), BF16)
    weights = pl.pallas_call(
        lambda *refs: weights_body(plane_total, *refs),
        out_shape=(small,) * 3,
        in_specs=[vmem, smem, smem],
        out_specs=(vmem,) * 3,
        name="weights",
    )(rec_weight, planes, rec_count)
    weights = (
        weights[0],
        lax.ppermute(weights[1], "slab", swap),
        lax.ppermute(weights[2], "slab", onward),
    )
    sent = []
    for chunk, records in zip(chunks, arrived):
        weights, parts = assembled(chunk, weights, *records)
        sent.append(parts)
    values = []
    token = qweight
    for chunk, parts in zip(chunks, sent):
        token, blocks_of = combined(chunk, token, *parts)
        values.append(blocks_of)
    gram = ()
    for at, value in enumerate(values):
        copies = slabs if at == len(values) - 1 else 1
        values[at], result = partial_gram(value, gram, copies)
        gram = (result,)
    grams = lax.all_to_all(gram[0], "slab", split_axis=0, concat_axis=0, tiled=True)
    factor = pl.pallas_call(
        lambda *refs: factor_body(kept, *refs),
        out_shape=jax.ShapeDtypeStruct((kept, columns, columns), F32),
        in_specs=[vmem],
        out_specs=vmem,
        compiler_params=PARAMS,
        name="factor",
    )(grams)
    spectra = jnp.concatenate(values, axis=3)
    spectra = spectra.reshape(freqs, kept, plane_total, variables, blocks, 2, points)
    spectra = jnp.transpose(spectra, (1, 0, 4, 5, 2, 3, 6))
    spectra = spectra.reshape(kept, freqs * blocks, 2, plane_total, variables, points)
    return (spectra, factor)


def solution(mesh):
    placed = (
        P("slab", None, None, "freq", None, None, None),
        P("slab", None, None),
        P("slab", None),
        P("slab", None, None, None),
        P("slab", None),
    )
    return jax.shard_map(
        body,
        mesh=mesh,
        in_specs=placed,
        out_specs=(P("freq", None, None, "slab", None, None), P("freq", None, None)),
        check_vma=False,
    )
```
